256 devices in a mesh: dp: 16 (over x, y_hi, core), fsdp: 16 (over y_lo, z).
Axes of the slice: x: 4, y: 4 (y_hi: 2, y_lo: 2; y = y_hi * 2 + y_lo), z: 8, core: 2. Of those that a mesh axis runs over, the one named last changes fastest.
Arguments:
- tokens: bfloat16 [8192, 2048], P('dp'), may hold values from -6 to 6
- expert_ids: int32 [8192, 2], P('dp'), may hold values from 0 to 7, as said below
- route_probs: float32 [8192, 2], P('dp'), may hold values from 0.1 to 1
- gate_w: bfloat16 [2, 2048, 7168], P(None, 'dp', 'fsdp'), may hold values from -0.125 to 0.125
- up_w: bfloat16 [2, 2048, 7168], P(None, 'dp', 'fsdp'), may hold values from -0.125 to 0.125
- down_w: bfloat16 [2, 7168, 2048], P(None, 'fsdp', 'dp'), may hold values from -0.0625 to 0.0625
- out_grad: bfloat16 [8192, 2048], P('dp'), may hold values from -6 to 6
Outputs:
- mixed: bfloat16 [8192, 2048], P('dp')
- token_grad: bfloat16 [8192, 2048], P('dp')
- gate_grad: bfloat16 [2, 2048, 7168], P(None, 'dp', 'fsdp')
- up_grad: bfloat16 [2, 2048, 7168], P(None, 'dp', 'fsdp')
- down_grad: bfloat16 [2, 7168, 2048], P(None, 'fsdp', 'dp')
The draws below stay inside these ranges and needn't reach their ends.
Inputs may be any that keep to these rules, and one draw needn't show every extreme that they name: `expert_ids`: the two entries of a row differ. In each aligned block of 512 rows (the rows of one index of dp) every expert is named by at most 256 rows, and one of experts 0 to 1 by exactly 256 rows.
All inputs are finite; a program needn't handle non-finite values.
Results may differ from the reference program's by a relative error of at most 0.018.
Values may be sent and summed in bfloat16 or wider, within the bound.
A program may use at most 128 MiB of HBM per device.

```python
import jax
import jax.numpy as jnp
from jax import lax

D = 2048
HID = 7168
NEXP = 8
EWIN = 2
TOPK = 2
TOK_DEV = 512
TOKENS = 8192


def draw_expert_ids(key, part):
    blocks = TOKENS // TOK_DEV
    half = TOK_DEV // 2
    others = NEXP - 1
    key_hot, key_perm, key_offset, key_swap = jax.random.split(key, 4)
    hot = jax.random.randint(key_hot, (blocks, 1), 0, EWIN).astype(jnp.int32)

    def one_perm(sub_key):
        return jax.random.permutation(sub_key, TOK_DEV)
    perms = jax.vmap(one_perm)(jax.random.split(key_perm, blocks)).astype(jnp.int32)
    ranking = jnp.argsort(perms, axis=1).astype(jnp.int32)
    offsets = jax.random.randint(key_offset, (blocks, 3), 0, others).astype(jnp.int32)
    is_hot = ranking < half
    first_index = (ranking + offsets[:, 0:1]) % others
    second_hot = (ranking + offsets[:, 1:2]) % others
    second_cold = (first_index + 1 + (ranking // others + offsets[:, 2:3]) % (others - 1)) % others

    def lifted(index):
        return index + (index >= hot).astype(jnp.int32)
    first = jnp.where(is_hot, hot, lifted(first_index))
    second = jnp.where(is_hot, lifted(second_hot), lifted(second_cold))
    swapped = jax.random.randint(key_swap, (blocks, TOK_DEV), 0, 2) == 1
    slot_first = jnp.where(swapped, second, first)
    slot_second = jnp.where(swapped, first, second)
    return jnp.stack([slot_first, slot_second], axis=-1).reshape(TOKENS, 2).astype(jnp.int32)


def steps_of(rng, extent, shards, smallest, largest):
    loudness, own = 1.0, jax.random.fold_in(rng, 6)
    for axis_at, blocks in shards:
        draws = jnp.exp(jax.random.uniform(jax.random.fold_in(own, axis_at), (blocks,), jnp.float32, smallest / len(shards), largest / len(shards)))
        loudness = loudness * jnp.repeat(draws, extent[axis_at] // blocks).reshape([-1 if axis == axis_at else 1 for axis in range(len(extent))])
    return loudness


def normal_values(stream_key, shape, scale, bound, shards=(), kind=jnp.bfloat16):
    drawn = scale * jax.random.normal(stream_key, shape, jnp.float32)
    if shards:
        drawn = drawn * steps_of(stream_key, shape, shards, -0.22, 0.18)
    return jnp.clip(drawn, -bound, bound).astype(kind)


def setup_inputs(seed: int = 0) -> dict:
    arg_keys = jax.random.split(jax.random.key(seed), 8)
    return {
        "tokens": normal_values(arg_keys[0], (TOKENS, D), 1.0, 6.0, ((0, 16),)),
        "expert_ids": draw_expert_ids(jax.random.fold_in(arg_keys[7], 71), 0),
        "route_probs": jnp.clip(0.1 + 0.9 * jax.random.uniform(arg_keys[2], (TOKENS, TOPK), jnp.float32) ** steps_of(arg_keys[2], (TOKENS, TOPK), ((0, 16),), -0.2, 0.2), 0.1, 1.0),
        "gate_w": normal_values(arg_keys[3], (EWIN, D, HID), D ** -0.5, 0.125, ((1, 16), (2, 16))),
        "up_w": normal_values(arg_keys[4], (EWIN, D, HID), D ** -0.5, 0.125, ((1, 16), (2, 16))),
        "down_w": normal_values(arg_keys[5], (EWIN, HID, D), HID ** -0.5, 0.0625, ((1, 16), (2, 16))),
        "out_grad": normal_values(arg_keys[6], (TOKENS, D), 1.0, 6.0, ((0, 16),)),
    }


def slot_layout(expert_ids, route_probs, expert, slot_cap):
    token_count = expert_ids.shape[0]
    matches = expert_ids == expert
    chosen = jnp.any(matches, axis=1)
    weight_token = jnp.sum(jnp.where(matches, route_probs, jnp.float32(0.0)), axis=1)
    position = (jnp.cumsum(chosen.astype(jnp.int32)) - 1).astype(jnp.int32)
    slot_index = lax.broadcasted_iota(jnp.int32, (slot_cap, token_count), 0)
    token_index = lax.broadcasted_iota(jnp.int32, (slot_cap, token_count), 1)
    matched_slots = (position[None, :] == slot_index) & chosen[None, :]
    slot_token = jnp.sum(jnp.where(matched_slots, token_index, 0), axis=1).astype(jnp.int32)
    slot_valid = jnp.any(matched_slots, axis=1)
    slot_weight = jnp.where(slot_valid, jnp.take(weight_token, slot_token), jnp.float32(0.0))
    token_slot = jnp.clip(position, 0, slot_cap - 1).astype(jnp.int32)
    return chosen, token_slot, slot_token, slot_valid, slot_weight


def expert_block(block_tokens, block_ids, block_probs, block_grad, expert, gate_full, up_full, down_full):
    slot_cap = block_tokens.shape[0] // 2
    chosen, token_slot, slot_token, slot_valid, slot_weight = slot_layout(block_ids, block_probs, expert, slot_cap)
    slot_input = jnp.take(block_tokens, slot_token, axis=0) * slot_valid[:, None].astype(block_tokens.dtype)
    gate_act = jnp.dot(slot_input, gate_full, preferred_element_type=jnp.float32)
    up_act = jnp.dot(slot_input, up_full, preferred_element_type=jnp.float32)
    hidden = (jax.nn.silu(gate_act) * up_act).astype(jnp.bfloat16)
    expert_out = jnp.dot(hidden, down_full, preferred_element_type=jnp.float32) * slot_weight[:, None]
    mixed_part = jnp.where(chosen[:, None], jnp.take(expert_out, token_slot, axis=0), jnp.float32(0.0))
    slot_grad = (jnp.take(block_grad, slot_token, axis=0).astype(jnp.float32) * slot_weight[:, None]).astype(jnp.bfloat16)
    down_term = lax.dot_general(hidden, slot_grad, (((0,), (0,)), ((), ())), preferred_element_type=jnp.float32)
    hidden_grad = lax.dot_general(slot_grad, down_full, (((1,), (1,)), ((), ())), preferred_element_type=jnp.float32)
    sigma = jax.nn.sigmoid(gate_act)
    up_act_grad = (hidden_grad * gate_act * sigma).astype(jnp.bfloat16)
    gate_act_grad = (hidden_grad * up_act * sigma * (1.0 + gate_act * (1.0 - sigma))).astype(jnp.bfloat16)
    gate_term = lax.dot_general(slot_input, gate_act_grad, (((0,), (0,)), ((), ())), preferred_element_type=jnp.float32)
    up_term = lax.dot_general(slot_input, up_act_grad, (((0,), (0,)), ((), ())), preferred_element_type=jnp.float32)
    input_grad = lax.dot_general(gate_act_grad, gate_full, (((1,), (1,)), ((), ())), preferred_element_type=jnp.float32)
    input_grad = input_grad + lax.dot_general(up_act_grad, up_full, (((1,), (1,)), ((), ())), preferred_element_type=jnp.float32)
    grad_part = jnp.where(chosen[:, None], jnp.take(input_grad, token_slot, axis=0), jnp.float32(0.0))
    return mixed_part, grad_part, gate_term, up_term, down_term


def reference(tokens, expert_ids, route_probs, gate_w, up_w, down_w, out_grad):
    blocks = TOKENS // TOK_DEV
    width = tokens.shape[1]
    block_inputs = (tokens.reshape(blocks, TOK_DEV, width), expert_ids.reshape(blocks, TOK_DEV, TOPK),
                    route_probs.reshape(blocks, TOK_DEV, TOPK), out_grad.reshape(blocks, TOK_DEV, width))

    def step(carry, inputs):
        block_tokens, block_ids, block_probs, block_grad = inputs
        gate_acc, up_acc, down_acc = carry
        mixed_sum = jnp.zeros((TOK_DEV, width), jnp.float32)
        grad_sum = jnp.zeros((TOK_DEV, width), jnp.float32)
        gate_list, up_list, down_list = [], [], []
        for expert in range(EWIN):
            mixed_part, grad_part, gate_term, up_term, down_term = expert_block(
                block_tokens, block_ids, block_probs, block_grad, expert, gate_w[expert], up_w[expert], down_w[expert])
            mixed_sum = mixed_sum + mixed_part
            grad_sum = grad_sum + grad_part
            gate_list.append(gate_term.astype(jnp.bfloat16).astype(jnp.float32))
            up_list.append(up_term.astype(jnp.bfloat16).astype(jnp.float32))
            down_list.append(down_term.astype(jnp.bfloat16).astype(jnp.float32))
        new_carry = (gate_acc + jnp.stack(gate_list), up_acc + jnp.stack(up_list), down_acc + jnp.stack(down_list))
        return new_carry, (mixed_sum.astype(jnp.bfloat16), grad_sum.astype(jnp.bfloat16))

    start = (jnp.zeros(gate_w.shape, jnp.float32), jnp.zeros(up_w.shape, jnp.float32), jnp.zeros(down_w.shape, jnp.float32))
    totals, outputs = lax.scan(step, start, block_inputs)
    mixed = outputs[0].reshape(TOKENS, width)
    token_grad = outputs[1].reshape(TOKENS, width)
    return (mixed, token_grad, totals[0].astype(jnp.bfloat16), totals[1].astype(jnp.bfloat16), totals[2].astype(jnp.bfloat16))
```

```python
import heapq

import jax
import jax.numpy as jnp
from jax import lax
from jax.experimental import pallas as pl
from jax.experimental.pallas import tpu as pltpu
from jax.sharding import PartitionSpec as P

MESH = pl.DeviceIdType.MESH
BF = jnp.bfloat16
F32 = jnp.float32
NX, NZ = 4, 8
LANE = 128
NSEM = 256

NT = (((1,), (1,)), ((), ()))
NN = (((1,), (0,)), ((), ()))
TN = (((0,), (0,)), ((), ()))


def dot(a, b, dims):
    return lax.dot_general(a, b, dims, preferred_element_type=F32)


class Clock:
    def __init__(self):
        self.heap, self.now, self.count = [], 0.0, 0

    def spawn(self, stream, delay=0.0):
        self.count += 1
        heapq.heappush(self.heap, (self.now + delay, self.count, stream))

    def busy(self, us):
        self.now += us

    def run(self):
        while self.heap:
            at, _, stream = heapq.heappop(self.heap)
            self.now = max(self.now, at)
            try:
                delay = next(stream)
            except StopIteration:
                continue
            self.spawn(stream, delay)


def add_into(out, terms, rows=64):
    lead = out.shape[:-2]
    total = 1
    for n in lead:
        total *= n
    height = out.shape[-2]
    while height % rows:
        rows //= 2
    steps = height // rows

    def step(i, carry):
        at, rest = lax.rem(i, steps), lax.div(i, steps)
        index = []
        for n in reversed(lead):
            index.append(lax.rem(rest, n))
            rest = lax.div(rest, n)
        index = tuple(reversed(index)) + (pl.ds(pl.multiple_of(at * rows, rows), rows), slice(None))
        value = terms[0][index].astype(F32)
        for term in terms[1:]:
            value = value + term[index].astype(F32)
        out[index] = value.astype(out.dtype)
        return carry

    lax.fori_loop(0, total * steps, step, 0)


def kernel(
    w_in, tok_ref, grad_ref, ids_ref, probs_ref,
    mixed_ref, tgrad_ref, wgrad_ref,
    w_all, dw, cr, xa, xb, ys, yr,
    a0, a1, z0, z1, y0s, y0r, y1r, s0, s1,
    pick, xin, gin, gt, ut, ht, gat, uat,
    send_sem, recv_sem, local_sem,
):
    dp, fs = lax.axis_index("dp"), lax.axis_index("fsdp")
    x, yh, c = dp // 4, (dp // 2) % 2, dp % 2
    yl, z = fs // NZ, fs % NZ
    experts, mats, hid, _ = w_in.shape
    tok, width = tok_ref.shape
    slots = tok // 2
    half = hid // 2
    core = (x * 4 + yh * 2 + 1 - c, fs)
    yhp = (x * 4 + (1 - yh) * 2 + c, fs)
    xr = (((x + 1) % NX) * 4 + yh * 2 + c, fs)
    xl = (((x + 3) % NX) * 4 + yh * 2 + c, fs)
    ylp = (dp, (1 - yl) * NZ + z)
    zr = (dp, yl * NZ + (z + 1) % NZ)
    zl = (dp, yl * NZ + (z + 7) % NZ)

    sent = []

    def send(src, dst, device):
        i = len(sent)
        copy = pltpu.make_async_remote_copy(
            src_ref=src, dst_ref=dst, send_sem=send_sem.at[i], recv_sem=recv_sem.at[i],
            device_id=device, device_id_type=MESH,
        )
        copy.start()
        sent.append(copy)
        return copy

    barrier = pltpu.get_barrier_semaphore()
    for peer in (core, yhp, xr, xl, ylp, zr, zl):
        pl.semaphore_signal(barrier, inc=1, device_id=peer, device_id_type=MESH)
    pl.semaphore_wait(barrier, 7)

    clock = Clock()

    from_core = [[] for _ in range(experts)]
    own_block = []

    def cols(block):
        return pl.ds(pl.multiple_of(block * LANE, LANE), LANE)

    def w_block(e, block, rows=slice(None)):
        return w_all.at[e, :, rows, cols(block)]

    def to_core(e, src, block, rows=slice(None)):
        from_core[e].append(send(src, w_block(e, block, rows), core))

    def gather_row(e, row, src):
        me = x * 4 + row * 2 + c
        left = ((x + 3) % NX) * 4 + row * 2 + c
        right = ((x + 1) % NX) * 4 + row * 2 + c
        far = ((x + 2) % NX) * 4 + row * 2 + c
        top, low = pl.ds(0, half), pl.ds(half, half)
        go_r = send(src, w_block(e, me), xr)
        go_l = send(src, w_block(e, me), xl)
        to_core(e, src, me)
        yield 9.0
        go_r.wait_recv()
        on_r = send(w_block(e, left, top), w_block(e, left, top), xr)
        to_core(e, w_block(e, left), left)
        yield 0.0
        go_l.wait_recv()
        on_l = send(w_block(e, right, low), w_block(e, right, low), xl)
        to_core(e, w_block(e, right), right)
        yield 6.0
        on_r.wait_recv()
        to_core(e, w_block(e, far, top), far, top)
        yield 0.0
        on_l.wait_recv()
        to_core(e, w_block(e, far, low), far, low)

    def gather_other(e, wait):
        copy = send(w_in.at[e], w_block(e, dp), yhp)
        yield wait
        copy.wait_recv()
        block = x * 4 + (1 - yh) * 2 + c
        yield from gather_row(e, 1 - yh, w_block(e, block))

    def scatter_grads(e):
        copies = {}
        for k in (2, 1, 3, 0):
            copies[k] = send(dw.at[e, 1 - c, (x + k) % NX], cr.at[e, k], core)
        yield 2.0

        def piece(k):
            return dw.at[e, c, (x + k) % NX]

        copies[2].wait_recv()
        add_into(piece(2), [piece(2), cr.at[e, 2]])
        top, low = pl.ds(0, half), pl.ds(half, half)
        far = (x + 2) % NX
        go_r = send(dw.at[e, c, far, :, :, top], xa.at[e, 0], xr)
        go_l = send(dw.at[e, c, far, :, :, low], xa.at[e, 1], xl)
        yield 1.0
        copies[1].wait_recv()
        add_into(piece(1), [piece(1), cr.at[e, 1]])
        yield 1.0
        copies[3].wait_recv()
        add_into(piece(3), [piece(3), cr.at[e, 3]])
        yield 6.0
        go_r.wait_recv()
        at = dw.at[e, c, (x + 1) % NX, :, :, top]
        add_into(at, [at, xa.at[e, 0]], 32)
        on_r = send(piece(1), xb.at[e, 0], xr)
        yield 0.0
        go_l.wait_recv()
        at = dw.at[e, c, (x + 3) % NX, :, :, low]
        add_into(at, [at, xa.at[e, 1]], 32)
        on_l = send(piece(3), xb.at[e, 1], xl)
        yield 1.0
        copies[0].wait_recv()
        yield 14.0
        on_r.wait_recv()
        on_l.wait_recv()
        other = 1 - yh
        add_into(ys.at[e], [piece(0).at[other], cr.at[e, 0, other], xb.at[e, 0, other], xb.at[e, 1, other]])
        last = send(ys.at[e], yr.at[e], yhp)
        yield 12.0
        last.wait_recv()
        add_into(
            wgrad_ref.at[e],
            [piece(0).at[yh], cr.at[e, 0, yh], xb.at[e, 0, yh], xb.at[e, 1, yh], yr.at[e]],
        )

    summed = [0, 0]

    def sum_outputs(e):
        def piece(k):
            return a0.at[e, (z + k) % NZ]

        h = NZ // 2
        go_r = send(piece(h).at[0], z0.at[e, 0, 0, 0], zr)
        go_l = send(piece(h).at[1], z0.at[e, 1, 0, 1], zl)
        for k in range(1, h):
            yield 3.0 if k == 1 else 5.0
            go_r.wait_recv()
            if k == 1:
                add_into(piece(h - k).at[0], [piece(h - k).at[0], z0.at[e, 0, 0, 0]])
            else:
                add_into(piece(h - k), [piece(h - k), z0.at[e, 0, k - 1]])
            go_r = send(piece(h - k), z0.at[e, 0, k], zr)
            go_l.wait_recv()
            if k == 1:
                add_into(piece(h + k).at[1], [piece(h + k).at[1], z0.at[e, 1, 0, 1]])
            else:
                add_into(piece(h + k), [piece(h + k), z0.at[e, 1, k - 1]])
            go_l = send(piece(h + k), z0.at[e, 1, k], zl)
        yield 5.0
        go_r.wait_recv()
        go_l.wait_recv()
        other = 1 - yl
        add_into(y0s.at[e], [piece(0).at[other], z0.at[e, 0, h - 1, other], z0.at[e, 1, h - 1, other]])
        last = send(y0s.at[e], y0r.at[e], ylp)
        yield 3.0
        last.wait_recv()
        add_into(s0.at[e], [piece(0).at[yl], z0.at[e, 0, h - 1, yl], z0.at[e, 1, h - 1, yl], y0r.at[e]])
        summed[0] += 1

    def sum_grads(e):
        def piece(k):
            return a1.at[e, yl, (z + k) % NZ]

        h = NZ // 2
        order = [h] + [k for i in range(1, h) for k in (h - i, h + i)] + [0]
        first = {}
        for k in order:
            first[k] = send(a1.at[e, 1 - yl, (z + k) % NZ], y1r.at[e, k], ylp)

        def take(k):
            first[k].wait_recv()
            add_into(piece(k), [piece(k), y1r.at[e, k]])

        yield 3.0
        take(h)
        hs = slots // 2
        top, low = pl.ds(0, hs), pl.ds(hs, hs)
        far = (z + h) % NZ
        go_r = send(a1.at[e, yl, far, top], z1.at[e, 0, 0, top], zr)
        go_l = send(a1.at[e, yl, far, low], z1.at[e, 1, 0, low], zl)
        for k in range(1, h):
            yield 3.0
            take(h - k)
            take(h + k)
            go_r.wait_recv()
            if k == 1:
                at = a1.at[e, yl, (z + h - k) % NZ, top]
                add_into(at, [at, z1.at[e, 0, 0, top]])
            else:
                add_into(piece(h - k), [piece(h - k), z1.at[e, 0, k - 1]])
            go_r = send(piece(h - k), z1.at[e, 0, k], zr)
            go_l.wait_recv()
            if k == 1:
                at = a1.at[e, yl, (z + h + k) % NZ, low]
                add_into(at, [at, z1.at[e, 1, 0, low]])
            else:
                add_into(piece(h + k), [piece(h + k), z1.at[e, 1, k - 1]])
            go_l = send(piece(h + k), z1.at[e, 1, k], zl)
        yield 3.0
        first[0].wait_recv()
        go_r.wait_recv()
        go_l.wait_recv()
        add_into(s1.at[e], [piece(0), y1r.at[e, 0], z1.at[e, 0, h - 1], z1.at[e, 1, h - 1]])
        summed[1] += 1

    def place(out, sums):
        value = dot(pick[0], sums[0], TN)
        for e in range(1, experts):
            value = value + dot(pick[e], sums[e], TN)
        out[:, cols(fs)] = value.astype(out.dtype)

    def share_outputs():
        while summed[0] < experts:
            yield 1.0
        place(mixed_ref, s0)

        def at(y, k):
            return mixed_ref.at[:, cols(y * NZ + (z + k) % NZ)]

        copy = send(at(yl, 0), at(yl, 0), ylp)
        yield 3.0
        copy.wait_recv()
        h = NZ // 2
        go_r = [send(at(y, 0), at(y, 0), zr) for y in range(2)]
        go_l = [send(at(y, 0), at(y, 0), zl) for y in range(2)]
        for k in range(1, h):
            yield 5.0
            for y in range(2):
                go_r[y].wait_recv()
                go_r[y] = send(at(y, -k + NZ), at(y, -k + NZ), zr) if k < h - 1 or y == 0 else None
                go_l[y].wait_recv()
                go_l[y] = send(at(y, k), at(y, k), zl) if k < h - 1 or y == 1 else None
        yield 4.0
        go_r[0].wait_recv()
        go_l[1].wait_recv()

    def share_grads():
        while summed[1] < experts:
            yield 1.0
        place(tgrad_ref, s1)
        ht_ = tok // 2
        top, low = pl.ds(0, ht_), pl.ds(ht_, ht_)

        def at(k, rows=slice(None)):
            return tgrad_ref.at[rows, cols(yl * NZ + (z + k) % NZ)]

        across = []

        def cross(k, rows=slice(None)):
            across.append(send(at(k, rows), at(k, rows), ylp))

        h = NZ // 2
        go_r, go_l = send(at(0), at(0), zr), send(at(0), at(0), zl)
        cross(0)
        for k in range(1, h):
            yield 3.0
            rows_r, rows_l = (slice(None), slice(None)) if k < h - 1 else (top, low)
            go_r.wait_recv()
            go_r = send(at(NZ - k, rows_r), at(NZ - k, rows_r), zr)
            cross(NZ - k)
            go_l.wait_recv()
            go_l = send(at(k, rows_l), at(k, rows_l), zl)
            cross(k)
        yield 3.0
        go_r.wait_recv()
        cross(h, top)
        go_l.wait_recv()
        cross(h, low)
        yield 4.0
        for copy in across:
            copy.wait_recv()

    def slot_rows(e):
        hit = ids_ref[...] == e
        chosen = jnp.max(hit.astype(F32), axis=0, keepdims=True)
        weight = jnp.sum(jnp.where(hit, probs_ref[...], 0.0), axis=0, keepdims=True)
        before = lax.broadcasted_iota(jnp.int32, (tok, tok), 0)
        after = lax.broadcasted_iota(jnp.int32, (tok, tok), 1)
        upper = (before <= after).astype(F32).astype(BF)
        count = dot(jnp.broadcast_to(chosen, (16, tok)).astype(BF), upper, NN)[0:1, :]
        place_of = jnp.where(chosen > 0.0, count - 1.0, -1.0).astype(jnp.int32)
        rows = lax.broadcasted_iota(jnp.int32, (slots, tok), 0)
        mine = (jnp.broadcast_to(place_of, (slots, tok)) == rows).astype(F32)
        slot_weight = jnp.sum(mine * weight, axis=1, keepdims=True)
        pick[e] = mine.astype(BF)
        return slot_weight

    part = 512

    def compute():
        weights = []
        for e in range(experts):
            weights.append(slot_rows(e))
            for j in range(0, width, part):
                at = pl.ds(j, part)
                xin[e, :, at] = dot(pick[e], tok_ref[:, at], NN).astype(BF)
                gin[e, :, at] = (dot(pick[e], grad_ref[:, at], NN) * weights[e]).astype(BF)
            clock.busy(3.0)
            yield 0.0
        for e in range(experts):
            while len(from_core[e]) < 10:
                yield 1.0
            yield 2.0
            own_block[e].wait()
            for copy in from_core[e]:
                copy.wait_recv()
            gt[...] = dot(w_all[e, 0], xin[e], NT)
            ut[...] = dot(w_all[e, 1], xin[e], NT)
            clock.busy(1.5)
            yield 0.0
            gate = gt[...]
            sig = 1.0 / (1.0 + jnp.exp(-gate))
            ht[...] = (gate * sig * ut[...]).astype(BF)
            for j in range(0, width, part):
                value = dot(ht[...], w_all[e, 2, :, pl.ds(j, part)], TN) * weights[e]
                for b in range(part // LANE):
                    f = j // LANE + b
                    a0[e, f % NZ, f // NZ] = value[:, b * LANE : (b + 1) * LANE].astype(BF)
            clock.busy(1.5)
            clock.spawn(sum_outputs(e))
            yield 0.0
            back = dot(w_all[e, 2], gin[e], NT)
            gate = gt[...]
            sig = 1.0 / (1.0 + jnp.exp(-gate))
            uat[...] = (back * gate * sig).astype(BF)
            gat[...] = (back * ut[...] * sig * (1.0 + gate * (1.0 - sig))).astype(BF)
            clock.busy(1.5)
            yield 0.0
            for j in range(0, width, part):
                at = pl.ds(j, part)
                value = dot(gat[...], w_all[e, 0, :, at], TN) + dot(uat[...], w_all[e, 1, :, at], TN)
                for b in range(part // LANE):
                    f = j // LANE + b
                    a1[e, f // NZ, f % NZ] = value[:, b * LANE : (b + 1) * LANE].astype(BF)
            clock.busy(1.5)
            clock.spawn(sum_grads(e))
            yield 0.0
            for j in range(0, width, part):
                at = pl.ds(j, part)
                for m, (left, right) in enumerate(((gat, xin), (uat, xin), (ht, gin))):
                    value = dot(left[...], right[e, :, at], NN)
                    for b in range(part // LANE):
                        d = j // LANE + b
                        dw[e, d % 2, d // 4, (d // 2) % 2, m] = value[:, b * LANE : (b + 1) * LANE].astype(BF)
                clock.busy(0.6)
                yield 0.0
            clock.spawn(scatter_grads(e))

    for e in range(experts):
        copy = pltpu.make_async_copy(w_in.at[e], w_block(e, dp), local_sem.at[e])
        copy.start()
        own_block.append(copy)
    clock.spawn(gather_row(0, yh, w_in.at[0]))
    clock.spawn(gather_other(0, 16.0))
    clock.spawn(gather_other(1, 31.0))
    clock.spawn(compute())
    clock.spawn(gather_row(1, yh, w_in.at[1]), 12.0)
    clock.spawn(share_outputs(), 60.0)
    clock.spawn(share_grads(), 60.0)
    clock.run()
    for copy in sent:
        copy.wait_send()
    assert len(sent) <= NSEM, len(sent)


def body(tokens, expert_ids, route_probs, gate_w, up_w, down_w, out_grad):
    tok, width = tokens.shape
    experts, rows, hid = gate_w.shape
    assert rows == LANE and tok == 512
    slots = tok // 2
    shard = jnp.stack([gate_w.swapaxes(1, 2), up_w.swapaxes(1, 2), down_w], axis=1)
    vmem = pl.BlockSpec(memory_space=pltpu.VMEM)
    two = experts
    scratch = [
        pltpu.VMEM((two, 3, hid, width), BF),
        pltpu.VMEM((two, 2, NX, 2, 3, hid, LANE), BF),
        pltpu.VMEM((two, NX, 2, 3, hid, LANE), BF),
        pltpu.VMEM((two, 2, 2, 3, hid // 2, LANE), BF),
        pltpu.VMEM((two, 2, 2, 3, hid, LANE), BF),
        pltpu.VMEM((two, 3, hid, LANE), BF),
        pltpu.VMEM((two, 3, hid, LANE), BF),
        pltpu.VMEM((two, NZ, 2, slots, LANE), BF),
        pltpu.VMEM((two, 2, NZ, slots, LANE), BF),
        pltpu.VMEM((two, 2, NZ // 2, 2, slots, LANE), BF),
        pltpu.VMEM((two, 2, NZ // 2, slots, LANE), BF),
        pltpu.VMEM((two, slots, LANE), BF),
        pltpu.VMEM((two, slots, LANE), BF),
        pltpu.VMEM((two, NZ, slots, LANE), BF),
        pltpu.VMEM((two, slots, LANE), BF),
        pltpu.VMEM((two, slots, LANE), BF),
        pltpu.VMEM((two, slots, tok), BF),
        pltpu.VMEM((two, slots, width), BF),
        pltpu.VMEM((two, slots, width), BF),
        pltpu.VMEM((hid, slots), F32),
        pltpu.VMEM((hid, slots), F32),
        pltpu.VMEM((hid, slots), BF),
        pltpu.VMEM((hid, slots), BF),
        pltpu.VMEM((hid, slots), BF),
        pltpu.SemaphoreType.DMA((NSEM,)),
        pltpu.SemaphoreType.DMA((NSEM,)),
        pltpu.SemaphoreType.DMA((2,)),
    ]
    mixed, token_grad, grads = pl.pallas_call(
        kernel,
        out_shape=(
            jax.ShapeDtypeStruct((tok, width), BF),
            jax.ShapeDtypeStruct((tok, width), BF),
            jax.ShapeDtypeStruct((experts, 3, hid, LANE), BF),
        ),
        in_specs=[vmem] * 5,
        out_specs=(vmem, vmem, vmem),
        scratch_shapes=scratch,
        compiler_params=pltpu.CompilerParams(
            collective_id=0, has_side_effects=True, vmem_limit_bytes=67_043_328
        ),
        name="moe_layer",
    )(shard, tokens, out_grad, expert_ids.T, route_probs.T)
    return (
        mixed,
        token_grad,
        grads[:, 0].swapaxes(1, 2),
        grads[:, 1].swapaxes(1, 2),
        grads[:, 2],
    )


def solution(mesh):
    placed = (
        P("dp", None),
        P("dp", None),
        P("dp", None),
        P(None, "dp", "fsdp"),
        P(None, "dp", "fsdp"),
        P(None, "fsdp", "dp"),
        P("dp", None),
    )
    return jax.shard_map(
        body,
        mesh=mesh,
        in_specs=placed,
        out_specs=(
            P("dp", None),
            P("dp", None),
            P(None, "dp", "fsdp"),
            P(None, "dp", "fsdp"),
            P(None, "fsdp", "dp"),
        ),
        check_vma=False,
    )
```

```python
import heapq

import jax
import jax.numpy as jnp
from jax import lax
from jax.experimental import pallas as pl
from jax.experimental.pallas import tpu as pltpu
from jax.sharding import PartitionSpec as P

MESH = pl.DeviceIdType.MESH
BF = jnp.bfloat16
F32 = jnp.float32
NX, NZ = 4, 8
LANE = 128
NSEM = 256

NT = (((1,), (1,)), ((), ()))
NN = (((1,), (0,)), ((), ()))
TN = (((0,), (0,)), ((), ()))


def dot(a, b, dims):
    return lax.dot_general(a, b, dims, preferred_element_type=F32)


class Clock:
    def __init__(self):
        self.heap, self.now, self.count = [], 0.0, 0

    def spawn(self, stream, delay=0.0):
        self.count += 1
        heapq.heappush(self.heap, (self.now + delay, self.count, stream))

    def busy(self, us):
        self.now += us

    def run(self):
        while self.heap:
            at, _, stream = heapq.heappop(self.heap)
            self.now = max(self.now, at)
            try:
                delay = next(stream)
            except StopIteration:
                continue
            self.spawn(stream, delay)


def add_into(out, terms, rows=64):
    lead = out.shape[:-2]
    total = 1
    for n in lead:
        total *= n
    height = out.shape[-2]
    while height % rows:
        rows //= 2
    steps = height // rows

    def step(i, carry):
        at, rest = lax.rem(i, steps), lax.div(i, steps)
        index = []
        for n in reversed(lead):
            index.append(lax.rem(rest, n))
            rest = lax.div(rest, n)
        index = tuple(reversed(index)) + (pl.ds(pl.multiple_of(at * rows, rows), rows), slice(None))
        value = terms[0][index].astype(F32)
        for term in terms[1:]:
            value = value + term[index].astype(F32)
        out[index] = value.astype(out.dtype)
        return carry

    lax.fori_loop(0, total * steps, step, 0)


def kernel(
    w_in, tok_ref, grad_ref, ids_ref, probs_ref,
    mixed_ref, tgrad_ref, wgrad_ref,
    w_all, dw, cr, xa, xb, ys, yr,
    a0, a1, z0, z1, y0s, y0r, y1r, s0, s1,
    m_all, t_all, pick, xin, gin, gt, ut, ht, gat, uat,
    send_sem, recv_sem, local_sem,
):
    dp, fs = lax.axis_index("dp"), lax.axis_index("fsdp")
    x, yh, c = dp // 4, (dp // 2) % 2, dp % 2
    yl, z = fs // NZ, fs % NZ
    experts, mats, hid, _ = w_in.shape
    tok, width = tok_ref.shape
    slots = tok // 2
    half = hid // 2
    core = (x * 4 + yh * 2 + 1 - c, fs)
    yhp = (x * 4 + (1 - yh) * 2 + c, fs)
    xr = (((x + 1) % NX) * 4 + yh * 2 + c, fs)
    xl = (((x + 3) % NX) * 4 + yh * 2 + c, fs)
    ylp = (dp, (1 - yl) * NZ + z)
    zr = (dp, yl * NZ + (z + 1) % NZ)
    zl = (dp, yl * NZ + (z + 7) % NZ)

    sent = []

    def send(src, dst, device):
        i = len(sent)
        copy = pltpu.make_async_remote_copy(
            src_ref=src, dst_ref=dst, send_sem=send_sem.at[i], recv_sem=recv_sem.at[i],
            device_id=device, device_id_type=MESH,
        )
        copy.start()
        sent.append(copy)
        return copy

    barrier = pltpu.get_barrier_semaphore()
    for peer in (core, yhp, xr, xl, ylp, zr, zl):
        pl.semaphore_signal(barrier, inc=1, device_id=peer, device_id_type=MESH)
    pl.semaphore_wait(barrier, 7)

    clock = Clock()

    from_core = [[] for _ in range(experts)]
    own_block = []

    def cols(block):
        return pl.ds(pl.multiple_of(block * LANE, LANE), LANE)

    def w_block(e, block, rows=slice(None)):
        return w_all.at[e, :, rows, cols(block)]

    def to_core(e, src, block, rows=slice(None)):
        from_core[e].append(send(src, w_block(e, block, rows), core))

    def gather_row(e, row, src):
        me = x * 4 + row * 2 + c
        left = ((x + 3) % NX) * 4 + row * 2 + c
        right = ((x + 1) % NX) * 4 + row * 2 + c
        far = ((x + 2) % NX) * 4 + row * 2 + c
        top, low = pl.ds(0, half), pl.ds(half, half)
        go_r = send(src, w_block(e, me), xr)
        go_l = send(src, w_block(e, me), xl)
        to_core(e, src, me)
        yield 9.0
        go_r.wait_recv()
        on_r = send(w_block(e, left, top), w_block(e, left, top), xr)
        to_core(e, w_block(e, left), left)
        yield 0.0
        go_l.wait_recv()
        on_l = send(w_block(e, right, low), w_block(e, right, low), xl)
        to_core(e, w_block(e, right), right)
        yield 6.0
        on_r.wait_recv()
        to_core(e, w_block(e, far, top), far, top)
        yield 0.0
        on_l.wait_recv()
        to_core(e, w_block(e, far, low), far, low)

    def gather_other(e, wait):
        copy = send(w_in.at[e], w_block(e, dp), yhp)
        yield wait
        copy.wait_recv()
        block = x * 4 + (1 - yh) * 2 + c
        yield from gather_row(e, 1 - yh, w_block(e, block))

    def scatter_grads(e):
        copies = {}
        for k in (2, 1, 3, 0):
            copies[k] = send(dw.at[e, 1 - c, (x + k) % NX], cr.at[e, k], core)
        yield 2.0

        def piece(k):
            return dw.at[e, c, (x + k) % NX]

        copies[2].wait_recv()
        add_into(piece(2), [piece(2), cr.at[e, 2]])
        top, low = pl.ds(0, half), pl.ds(half, half)
        far = (x + 2) % NX
        go_r = send(dw.at[e, c, far, :, :, top], xa.at[e, 0], xr)
        go_l = send(dw.at[e, c, far, :, :, low], xa.at[e, 1], xl)
        yield 1.0
        copies[1].wait_recv()
        add_into(piece(1), [piece(1), cr.at[e, 1]])
        yield 1.0
        copies[3].wait_recv()
        add_into(piece(3), [piece(3), cr.at[e, 3]])
        yield 6.0
        go_r.wait_recv()
        at = dw.at[e, c, (x + 1) % NX, :, :, top]
        add_into(at, [at, xa.at[e, 0]], 32)
        on_r = send(piece(1), xb.at[e, 0], xr)
        yield 0.0
        go_l.wait_recv()
        at = dw.at[e, c, (x + 3) % NX, :, :, low]
        add_into(at, [at, xa.at[e, 1]], 32)
        on_l = send(piece(3), xb.at[e, 1], xl)
        yield 1.0
        copies[0].wait_recv()
        yield 14.0
        on_r.wait_recv()
        on_l.wait_recv()
        other = 1 - yh
        add_into(ys.at[e], [piece(0).at[other], cr.at[e, 0, other], xb.at[e, 0, other], xb.at[e, 1, other]])
        last = send(ys.at[e], yr.at[e], yhp)
        yield 12.0
        last.wait_recv()
        add_into(
            wgrad_ref.at[e],
            [piece(0).at[yh], cr.at[e, 0, yh], xb.at[e, 0, yh], xb.at[e, 1, yh], yr.at[e]],
        )

    shared = [0, 0]

    def sum_outputs(e):
        def piece(k):
            return a0.at[e, (z + k) % NZ]

        h = NZ // 2
        go_r = send(piece(h).at[0], z0.at[e, 0, 0, 0], zr)
        go_l = send(piece(h).at[1], z0.at[e, 1, 0, 1], zl)
        for k in range(1, h):
            yield 3.0 if k == 1 else 5.0
            go_r.wait_recv()
            if k == 1:
                add_into(piece(h - k).at[0], [piece(h - k).at[0], z0.at[e, 0, 0, 0]])
            else:
                add_into(piece(h - k), [piece(h - k), z0.at[e, 0, k - 1]])
            go_r = send(piece(h - k), z0.at[e, 0, k], zr)
            go_l.wait_recv()
            if k == 1:
                add_into(piece(h + k).at[1], [piece(h + k).at[1], z0.at[e, 1, 0, 1]])
            else:
                add_into(piece(h + k), [piece(h + k), z0.at[e, 1, k - 1]])
            go_l = send(piece(h + k), z0.at[e, 1, k], zl)
        yield 5.0
        go_r.wait_recv()
        go_l.wait_recv()
        other = 1 - yl
        add_into(y0s.at[e], [piece(0).at[other], z0.at[e, 0, h - 1, other], z0.at[e, 1, h - 1, other]])
        last = send(y0s.at[e], y0r.at[e], ylp)
        yield 3.0
        last.wait_recv()
        add_into(s0.at[e], [piece(0).at[yl], z0.at[e, 0, h - 1, yl], z0.at[e, 1, h - 1, yl], y0r.at[e]])
        m_all[e, :, cols(fs)] = s0[e]
        clock.spawn(share_outputs(e))

    def sum_grads(e):
        def piece(k):
            return a1.at[e, yl, (z + k) % NZ]

        h = NZ // 2
        order = [h] + [k for i in range(1, h) for k in (h - i, h + i)] + [0]
        first = {}
        for k in order:
            first[k] = send(a1.at[e, 1 - yl, (z + k) % NZ], y1r.at[e, k], ylp)

        def take(k):
            first[k].wait_recv()
            add_into(piece(k), [piece(k), y1r.at[e, k]])

        yield 3.0
        take(h)
        hs = slots // 2
        top, low = pl.ds(0, hs), pl.ds(hs, hs)
        far = (z + h) % NZ
        go_r = send(a1.at[e, yl, far, top], z1.at[e, 0, 0, top], zr)
        go_l = send(a1.at[e, yl, far, low], z1.at[e, 1, 0, low], zl)
        for k in range(1, h):
            yield 3.0
            take(h - k)
            take(h + k)
            go_r.wait_recv()
            if k == 1:
                at = a1.at[e, yl, (z + h - k) % NZ, top]
                add_into(at, [at, z1.at[e, 0, 0, top]])
            else:
                add_into(piece(h - k), [piece(h - k), z1.at[e, 0, k - 1]])
            go_r = send(piece(h - k), z1.at[e, 0, k], zr)
            go_l.wait_recv()
            if k == 1:
                at = a1.at[e, yl, (z + h + k) % NZ, low]
                add_into(at, [at, z1.at[e, 1, 0, low]])
            else:
                add_into(piece(h + k), [piece(h + k), z1.at[e, 1, k - 1]])
            go_l = send(piece(h + k), z1.at[e, 1, k], zl)
        yield 3.0
        first[0].wait_recv()
        go_r.wait_recv()
        go_l.wait_recv()
        add_into(s1.at[e], [piece(0), y1r.at[e, 0], z1.at[e, 0, h - 1], z1.at[e, 1, h - 1]])
        t_all[e, :, cols(fs)] = s1[e]
        clock.spawn(share_grads(e))

    def place(out, sums):
        for j in range(0, width, part):
            at = pl.ds(j, part)
            value = dot(pick[0], sums[0, :, at], TN)
            for e in range(1, experts):
                value = value + dot(pick[e], sums[e, :, at], TN)
            out[:, at] = value.astype(out.dtype)

    def share_outputs(e):
        def at(y, k):
            return m_all.at[e, :, cols(y * NZ + (z + k) % NZ)]

        copy = send(s0.at[e], at(yl, 0), ylp)
        h = NZ // 2
        go_r, go_l = {}, {}
        go_r[0] = send(s0.at[e], at(yl, 0), zr)
        go_l[0] = send(s0.at[e], at(yl, 0), zl)
        yield 2.0
        copy.wait_recv()
        go_r[1] = send(at(1 - yl, 0), at(1 - yl, 0), zr)
        go_l[1] = send(at(1 - yl, 0), at(1 - yl, 0), zl)
        top, low = pl.ds(0, slots // 2), pl.ds(slots // 2, slots // 2)
        for k in range(1, h):
            yield 3.0
            for i, y in enumerate((yl, 1 - yl)):
                rows_r, rows_l = (slice(None), slice(None)) if k < h - 1 else (top, low)
                go_r[i].wait_recv()
                src = at(y, NZ - k).at[rows_r]
                go_r[i] = send(src, src, zr)
                go_l[i].wait_recv()
                src = at(y, k).at[rows_l]
                go_l[i] = send(src, src, zl)
        yield 3.0
        for i in range(2):
            go_r[i].wait_recv()
            go_l[i].wait_recv()
        shared[0] += 1
        if shared[0] == experts:
            place(mixed_ref, m_all)

    def share_grads(e):
        top, low = pl.ds(0, slots // 2), pl.ds(slots // 2, slots // 2)

        def at(k, rows=slice(None)):
            return t_all.at[e, rows, cols(yl * NZ + (z + k) % NZ)]

        across = []

        def cross(k, rows=slice(None)):
            across.append(send(at(k, rows), at(k, rows), ylp))

        h = NZ // 2
        go_r, go_l = send(s1.at[e], at(0), zr), send(s1.at[e], at(0), zl)
        across.append(send(s1.at[e], at(0), ylp))
        for k in range(1, h):
            yield 2.0
            rows_r, rows_l = (slice(None), slice(None)) if k < h - 1 else (top, low)
            go_r.wait_recv()
            go_r = send(at(NZ - k, rows_r), at(NZ - k, rows_r), zr)
            cross(NZ - k)
            go_l.wait_recv()
            go_l = send(at(k, rows_l), at(k, rows_l), zl)
            cross(k)
        yield 2.0
        go_r.wait_recv()
        cross(h, top)
        go_l.wait_recv()
        cross(h, low)
        yield 3.0
        for copy in across:
            copy.wait_recv()
        shared[1] += 1
        if shared[1] == experts:
            place(tgrad_ref, t_all)

    def slot_rows(e):
        hit = ids_ref[...] == e
        chosen = jnp.max(hit.astype(F32), axis=0, keepdims=True)
        weight = jnp.sum(jnp.where(hit, probs_ref[...], 0.0), axis=0, keepdims=True)
        before = lax.broadcasted_iota(jnp.int32, (tok, tok), 0)
        after = lax.broadcasted_iota(jnp.int32, (tok, tok), 1)
        upper = (before <= after).astype(F32).astype(BF)
        count = dot(jnp.broadcast_to(chosen, (16, tok)).astype(BF), upper, NN)[0:1, :]
        place_of = jnp.where(chosen > 0.0, count - 1.0, -1.0).astype(jnp.int32)
        rows = lax.broadcasted_iota(jnp.int32, (slots, tok), 0)
        mine = (jnp.broadcast_to(place_of, (slots, tok)) == rows).astype(F32)
        slot_weight = jnp.sum(mine * weight, axis=1, keepdims=True)
        pick[e] = mine.astype(BF)
        return slot_weight

    part = 512

    def compute():
        weights = []
        for e in range(experts):
            weights.append(slot_rows(e))
            for j in range(0, width, part):
                at = pl.ds(j, part)
                xin[e, :, at] = dot(pick[e], tok_ref[:, at], NN).astype(BF)
                gin[e, :, at] = (dot(pick[e], grad_ref[:, at], NN) * weights[e]).astype(BF)
            clock.busy(3.0)
            yield 0.0
        for e in range(experts):
            while len(from_core[e]) < 10:
                yield 1.0
            yield 2.0
            own_block[e].wait()
            for copy in from_core[e]:
                copy.wait_recv()
            gt[...] = dot(w_all[e, 0], xin[e], NT)
            ut[...] = dot(w_all[e, 1], xin[e], NT)
            clock.busy(1.5)
            yield 0.0
            gate = gt[...]
            sig = 1.0 / (1.0 + jnp.exp(-gate))
            ht[...] = (gate * sig * ut[...]).astype(BF)
            for j in range(0, width, part):
                value = dot(ht[...], w_all[e, 2, :, pl.ds(j, part)], TN) * weights[e]
                for b in range(part // LANE):
                    f = j // LANE + b
                    a0[e, f % NZ, f // NZ] = value[:, b * LANE : (b + 1) * LANE].astype(BF)
            clock.busy(1.5)
            clock.spawn(sum_outputs(e))
            yield 0.0
            back = dot(w_all[e, 2], gin[e], NT)
            gate = gt[...]
            sig = 1.0 / (1.0 + jnp.exp(-gate))
            uat[...] = (back * gate * sig).astype(BF)
            gat[...] = (back * ut[...] * sig * (1.0 + gate * (1.0 - sig))).astype(BF)
            clock.busy(1.5)
            yield 0.0
            for j in range(0, width, part):
                at = pl.ds(j, part)
                value = dot(gat[...], w_all[e, 0, :, at], TN) + dot(uat[...], w_all[e, 1, :, at], TN)
                for b in range(part // LANE):
                    f = j // LANE + b
                    a1[e, f // NZ, f % NZ] = value[:, b * LANE : (b + 1) * LANE].astype(BF)
            clock.busy(1.5)
            clock.spawn(sum_grads(e))
            yield 0.0
            for j in range(0, width, part):
                at = pl.ds(j, part)
                for m, (left, right) in enumerate(((gat, xin), (uat, xin), (ht, gin))):
                    value = dot(left[...], right[e, :, at], NN)
                    for b in range(part // LANE):
                        d = j // LANE + b
                        dw[e, d % 2, d // 4, (d // 2) % 2, m] = value[:, b * LANE : (b + 1) * LANE].astype(BF)
                clock.busy(0.6)
                yield 0.0
            clock.spawn(scatter_grads(e))

    for e in range(experts):
        copy = pltpu.make_async_copy(w_in.at[e], w_block(e, dp), local_sem.at[e])
        copy.start()
        own_block.append(copy)
    clock.spawn(gather_row(0, yh, w_in.at[0]))
    clock.spawn(gather_other(0, 16.0))
    clock.spawn(gather_other(1, 31.0))
    clock.spawn(compute())
    clock.spawn(gather_row(1, yh, w_in.at[1]), 12.0)
    clock.run()
    for copy in sent:
        copy.wait_send()
    assert len(sent) <= NSEM, len(sent)


def body(tokens, expert_ids, route_probs, gate_w, up_w, down_w, out_grad):
    tok, width = tokens.shape
    experts, rows, hid = gate_w.shape
    assert rows == LANE and tok == 512
    slots = tok // 2
    shard = jnp.stack([gate_w.swapaxes(1, 2), up_w.swapaxes(1, 2), down_w], axis=1)
    vmem = pl.BlockSpec(memory_space=pltpu.VMEM)
    two = experts
    scratch = [
        pltpu.VMEM((two, 3, hid, width), BF),
        pltpu.VMEM((two, 2, NX, 2, 3, hid, LANE), BF),
        pltpu.VMEM((two, NX, 2, 3, hid, LANE), BF),
        pltpu.VMEM((two, 2, 2, 3, hid // 2, LANE), BF),
        pltpu.VMEM((two, 2, 2, 3, hid, LANE), BF),
        pltpu.VMEM((two, 3, hid, LANE), BF),
        pltpu.VMEM((two, 3, hid, LANE), BF),
        pltpu.VMEM((two, NZ, 2, slots, LANE), BF),
        pltpu.VMEM((two, 2, NZ, slots, LANE), BF),
        pltpu.VMEM((two, 2, NZ // 2, 2, slots, LANE), BF),
        pltpu.VMEM((two, 2, NZ // 2, slots, LANE), BF),
        pltpu.VMEM((two, slots, LANE), BF),
        pltpu.VMEM((two, slots, LANE), BF),
        pltpu.VMEM((two, NZ, slots, LANE), BF),
        pltpu.VMEM((two, slots, LANE), BF),
        pltpu.VMEM((two, slots, LANE), BF),
        pltpu.VMEM((two, slots, width), BF),
        pltpu.VMEM((two, slots, width), BF),
        pltpu.VMEM((two, slots, tok), BF),
        pltpu.VMEM((two, slots, width), BF),
        pltpu.VMEM((two, slots, width), BF),
        pltpu.VMEM((hid, slots), F32),
        pltpu.VMEM((hid, slots), F32),
        pltpu.VMEM((hid, slots), BF),
        pltpu.VMEM((hid, slots), BF),
        pltpu.VMEM((hid, slots), BF),
        pltpu.SemaphoreType.DMA((NSEM,)),
        pltpu.SemaphoreType.DMA((NSEM,)),
        pltpu.SemaphoreType.DMA((2,)),
    ]
    mixed, token_grad, grads = pl.pallas_call(
        kernel,
        out_shape=(
            jax.ShapeDtypeStruct((tok, width), BF),
            jax.ShapeDtypeStruct((tok, width), BF),
            jax.ShapeDtypeStruct((experts, 3, hid, LANE), BF),
        ),
        in_specs=[vmem] * 5,
        out_specs=(vmem, vmem, vmem),
        scratch_shapes=scratch,
        compiler_params=pltpu.CompilerParams(
            collective_id=0, has_side_effects=True, vmem_limit_bytes=67_043_328
        ),
        name="moe_layer",
    )(shard, tokens, out_grad, expert_ids.T, route_probs.T)
    return (
        mixed,
        token_grad,
        grads[:, 0].swapaxes(1, 2),
        grads[:, 1].swapaxes(1, 2),
        grads[:, 2],
    )


def solution(mesh):
    placed = (
        P("dp", None),
        P("dp", None),
        P("dp", None),
        P(None, "dp", "fsdp"),
        P(None, "dp", "fsdp"),
        P(None, "fsdp", "dp"),
        P("dp", None),
    )
    return jax.shard_map(
        body,
        mesh=mesh,
        in_specs=placed,
        out_specs=(
            P("dp", None),
            P("dp", None),
            P(None, "dp", "fsdp"),
            P(None, "dp", "fsdp"),
            P(None, "fsdp", "dp"),
        ),
        check_vma=False,
    )
```

```python
import heapq

import jax
import jax.numpy as jnp
from jax import lax
from jax.experimental import pallas as pl
from jax.experimental.pallas import tpu as pltpu
from jax.sharding import PartitionSpec as P

MESH = pl.DeviceIdType.MESH
BF = jnp.bfloat16
F32 = jnp.float32
NX, NZ = 4, 8
LANE = 128
NSEM = 256

NT = (((1,), (1,)), ((), ()))
NN = (((1,), (0,)), ((), ()))
TN = (((0,), (0,)), ((), ()))


def dot(a, b, dims):
    return lax.dot_general(a, b, dims, preferred_element_type=F32)


class Clock:
    def __init__(self):
        self.heap, self.now, self.count = [], 0.0, 0

    def spawn(self, stream, delay=0.0):
        self.count += 1
        heapq.heappush(self.heap, (self.now + delay, self.count, stream))

    def busy(self, us):
        self.now += us

    def run(self):
        while self.heap:
            at, _, stream = heapq.heappop(self.heap)
            self.now = max(self.now, at)
            try:
                delay = next(stream)
            except StopIteration:
                continue
            self.spawn(stream, delay)


def add_into(out, terms, rows=64):
    lead = out.shape[:-2]
    total = 1
    for n in lead:
        total *= n
    height = out.shape[-2]
    while height % rows:
        rows //= 2
    steps = height // rows

    def step(i, carry):
        at, rest = lax.rem(i, steps), lax.div(i, steps)
        index = []
        for n in reversed(lead):
            index.append(lax.rem(rest, n))
            rest = lax.div(rest, n)
        index = tuple(reversed(index)) + (pl.ds(pl.multiple_of(at * rows, rows), rows), slice(None))
        value = terms[0][index].astype(F32)
        for term in terms[1:]:
            value = value + term[index].astype(F32)
        out[index] = value.astype(out.dtype)
        return carry

    lax.fori_loop(0, total * steps, step, 0)


def kernel(
    w_in, tok_ref, grad_ref, ids_ref, probs_ref,
    mixed_ref, tgrad_ref, wgrad_ref,
    w_all, dw, cr, xa, xb, ys, yr,
    a0, a1, z0, z1, y0s, y0r, y1r, s0, s1,
    m_all, t_all, pick, xin, gin, gt, ut, ht, gat, uat,
    send_sem, recv_sem, local_sem,
):
    dp, fs = lax.axis_index("dp"), lax.axis_index("fsdp")
    x, yh, c = dp // 4, (dp // 2) % 2, dp % 2
    yl, z = fs // NZ, fs % NZ
    experts, mats, hid, _ = w_in.shape
    tok, width = tok_ref.shape
    slots = tok // 2
    half = hid // 2
    core = (x * 4 + yh * 2 + 1 - c, fs)
    yhp = (x * 4 + (1 - yh) * 2 + c, fs)
    xr = (((x + 1) % NX) * 4 + yh * 2 + c, fs)
    xl = (((x + 3) % NX) * 4 + yh * 2 + c, fs)
    ylp = (dp, (1 - yl) * NZ + z)
    zr = (dp, yl * NZ + (z + 1) % NZ)
    zl = (dp, yl * NZ + (z + 7) % NZ)

    sent = []

    def send(src, dst, device):
        i = len(sent)
        copy = pltpu.make_async_remote_copy(
            src_ref=src, dst_ref=dst, send_sem=send_sem.at[i], recv_sem=recv_sem.at[i],
            device_id=device, device_id_type=MESH,
        )
        copy.start()
        sent.append(copy)
        return copy

    barrier = pltpu.get_barrier_semaphore()
    for peer in (core, yhp, xr, xl, ylp, zr, zl):
        pl.semaphore_signal(barrier, inc=1, device_id=peer, device_id_type=MESH)
    pl.semaphore_wait(barrier, 7)

    clock = Clock()

    from_core = [[] for _ in range(experts)]
    own_block = []

    def cols(block):
        return pl.ds(pl.multiple_of(block * LANE, LANE), LANE)

    def w_block(e, block, rows=slice(None)):
        return w_all.at[e, :, rows, cols(block)]

    def to_core(e, src, block, rows=slice(None)):
        from_core[e].append(send(src, w_block(e, block, rows), core))

    def gather_row(e, row, src):
        me = x * 4 + row * 2 + c
        left = ((x + 3) % NX) * 4 + row * 2 + c
        right = ((x + 1) % NX) * 4 + row * 2 + c
        far = ((x + 2) % NX) * 4 + row * 2 + c
        top, low = pl.ds(0, half), pl.ds(half, half)
        go_r = send(src, w_block(e, me), xr)
        go_l = send(src, w_block(e, me), xl)
        to_core(e, src, me)
        yield 9.0
        go_r.wait_recv()
        on_r = send(w_block(e, left, top), w_block(e, left, top), xr)
        to_core(e, w_block(e, left), left)
        yield 0.0
        go_l.wait_recv()
        on_l = send(w_block(e, right, low), w_block(e, right, low), xl)
        to_core(e, w_block(e, right), right)
        yield 6.0
        on_r.wait_recv()
        to_core(e, w_block(e, far, top), far, top)
        yield 0.0
        on_l.wait_recv()
        to_core(e, w_block(e, far, low), far, low)

    def gather_other(e, wait):
        copy = send(w_in.at[e], w_block(e, dp), yhp)
        yield wait
        copy.wait_recv()
        block = x * 4 + (1 - yh) * 2 + c
        yield from gather_row(e, 1 - yh, w_block(e, block))

    def scatter_grads(e):
        copies = {}
        for k in (2, 1, 3, 0):
            copies[k] = send(dw.at[e, 1 - c, (x + k) % NX], cr.at[e, k], core)
        yield 2.0

        def piece(k):
            return dw.at[e, c, (x + k) % NX]

        copies[2].wait_recv()
        add_into(piece(2), [piece(2), cr.at[e, 2]])
        top, low = pl.ds(0, half), pl.ds(half, half)
        far = (x + 2) % NX
        go_r = send(dw.at[e, c, far, :, :, top], xa.at[e, 0], xr)
        go_l = send(dw.at[e, c, far, :, :, low], xa.at[e, 1], xl)
        yield 1.0
        copies[1].wait_recv()
        add_into(piece(1), [piece(1), cr.at[e, 1]])
        yield 1.0
        copies[3].wait_recv()
        add_into(piece(3), [piece(3), cr.at[e, 3]])
        yield 4.0
        go_r.wait_recv()
        at = dw.at[e, c, (x + 1) % NX, :, :, top]
        add_into(at, [at, xa.at[e, 0]], 32)
        on_r = send(piece(1), xb.at[e, 0], xr)
        yield 0.0
        go_l.wait_recv()
        at = dw.at[e, c, (x + 3) % NX, :, :, low]
        add_into(at, [at, xa.at[e, 1]], 32)
        on_l = send(piece(3), xb.at[e, 1], xl)
        yield 1.0
        copies[0].wait_recv()
        yield 10.0
        on_r.wait_recv()
        on_l.wait_recv()
        other = 1 - yh
        add_into(ys.at[e], [piece(0).at[other], cr.at[e, 0, other], xb.at[e, 0, other], xb.at[e, 1, other]])
        last = send(ys.at[e], yr.at[e], yhp)
        yield 12.0
        last.wait_recv()
        add_into(
            wgrad_ref.at[e],
            [piece(0).at[yh], cr.at[e, 0, yh], xb.at[e, 0, yh], xb.at[e, 1, yh], yr.at[e]],
        )

    shared = [0, 0]

    def sum_outputs(e):
        def piece(k):
            return a0.at[e, (z + k) % NZ]

        h = NZ // 2
        go_r = send(piece(h).at[0], z0.at[e, 0, 0, 0], zr)
        go_l = send(piece(h).at[1], z0.at[e, 1, 0, 1], zl)
        for k in range(1, h):
            yield 3.0 if k == 1 else 5.0
            go_r.wait_recv()
            if k == 1:
                add_into(piece(h - k).at[0], [piece(h - k).at[0], z0.at[e, 0, 0, 0]])
            else:
                add_into(piece(h - k), [piece(h - k), z0.at[e, 0, k - 1]])
            go_r = send(piece(h - k), z0.at[e, 0, k], zr)
            go_l.wait_recv()
            if k == 1:
                add_into(piece(h + k).at[1], [piece(h + k).at[1], z0.at[e, 1, 0, 1]])
            else:
                add_into(piece(h + k), [piece(h + k), z0.at[e, 1, k - 1]])
            go_l = send(piece(h + k), z0.at[e, 1, k], zl)
        yield 5.0
        go_r.wait_recv()
        go_l.wait_recv()
        other = 1 - yl
        add_into(y0s.at[e], [piece(0).at[other], z0.at[e, 0, h - 1, other], z0.at[e, 1, h - 1, other]])
        last = send(y0s.at[e], y0r.at[e], ylp)
        yield 3.0
        last.wait_recv()
        add_into(s0.at[e], [piece(0).at[yl], z0.at[e, 0, h - 1, yl], z0.at[e, 1, h - 1, yl], y0r.at[e]])
        m_all[e, :, cols(fs)] = s0[e]
        clock.spawn(share_outputs(e))

    def sum_grads(e):
        def piece(k):
            return a1.at[e, yl, (z + k) % NZ]

        h = NZ // 2
        order = [h] + [k for i in range(1, h) for k in (h - i, h + i)] + [0]
        first = {}
        for k in order:
            first[k] = send(a1.at[e, 1 - yl, (z + k) % NZ], y1r.at[e, k], ylp)

        def take(k):
            first[k].wait_recv()
            add_into(piece(k), [piece(k), y1r.at[e, k]])

        yield 3.0
        take(h)
        hs = slots // 2
        top, low = pl.ds(0, hs), pl.ds(hs, hs)
        far = (z + h) % NZ
        go_r = send(a1.at[e, yl, far, top], z1.at[e, 0, 0, top], zr)
        go_l = send(a1.at[e, yl, far, low], z1.at[e, 1, 0, low], zl)
        for k in range(1, h):
            yield 3.0
            take(h - k)
            take(h + k)
            go_r.wait_recv()
            if k == 1:
                at = a1.at[e, yl, (z + h - k) % NZ, top]
                add_into(at, [at, z1.at[e, 0, 0, top]])
            else:
                add_into(piece(h - k), [piece(h - k), z1.at[e, 0, k - 1]])
            go_r = send(piece(h - k), z1.at[e, 0, k], zr)
            go_l.wait_recv()
            if k == 1:
                at = a1.at[e, yl, (z + h + k) % NZ, low]
                add_into(at, [at, z1.at[e, 1, 0, low]])
            else:
                add_into(piece(h + k), [piece(h + k), z1.at[e, 1, k - 1]])
            go_l = send(piece(h + k), z1.at[e, 1, k], zl)
        yield 3.0
        first[0].wait_recv()
        go_r.wait_recv()
        go_l.wait_recv()
        add_into(s1.at[e], [piece(0), y1r.at[e, 0], z1.at[e, 0, h - 1], z1.at[e, 1, h - 1]])
        t_all[e, :, cols(fs)] = s1[e]
        clock.spawn(share_grads(e))

    def place(out, sums):
        for j in range(0, width, part):
            at = pl.ds(j, part)
            value = dot(pick[0], sums[0, :, at], TN)
            for e in range(1, experts):
                value = value + dot(pick[e], sums[e, :, at], TN)
            out[:, at] = value.astype(out.dtype)

    def share_outputs(e):
        def at(y, k):
            return m_all.at[e, :, cols(y * NZ + (z + k) % NZ)]

        copy = send(s0.at[e], at(yl, 0), ylp)
        h = NZ // 2
        go_r, go_l = {}, {}
        go_r[0] = send(s0.at[e], at(yl, 0), zr)
        go_l[0] = send(s0.at[e], at(yl, 0), zl)
        yield 2.0
        copy.wait_recv()
        go_r[1] = send(at(1 - yl, 0), at(1 - yl, 0), zr)
        go_l[1] = send(at(1 - yl, 0), at(1 - yl, 0), zl)
        top, low = pl.ds(0, slots // 2), pl.ds(slots // 2, slots // 2)
        for k in range(1, h):
            yield 3.0
            for i, y in enumerate((yl, 1 - yl)):
                rows_r, rows_l = (slice(None), slice(None)) if k < h - 1 else (top, low)
                go_r[i].wait_recv()
                src = at(y, NZ - k).at[rows_r]
                go_r[i] = send(src, src, zr)
                go_l[i].wait_recv()
                src = at(y, k).at[rows_l]
                go_l[i] = send(src, src, zl)
        yield 3.0
        for i in range(2):
            go_r[i].wait_recv()
            go_l[i].wait_recv()
        shared[0] += 1
        if shared[0] == experts:
            place(mixed_ref, m_all)

    def share_grads(e):
        top, low = pl.ds(0, slots // 2), pl.ds(slots // 2, slots // 2)

        def at(k, rows=slice(None)):
            return t_all.at[e, rows, cols(yl * NZ + (z + k) % NZ)]

        across = []

        def cross(k, rows=slice(None)):
            across.append(send(at(k, rows), at(k, rows), ylp))

        h = NZ // 2
        go_r, go_l = send(s1.at[e], at(0), zr), send(s1.at[e], at(0), zl)
        across.append(send(s1.at[e], at(0), ylp))
        for k in range(1, h):
            yield 2.0
            rows_r, rows_l = (slice(None), slice(None)) if k < h - 1 else (top, low)
            go_r.wait_recv()
            go_r = send(at(NZ - k, rows_r), at(NZ - k, rows_r), zr)
            cross(NZ - k)
            go_l.wait_recv()
            go_l = send(at(k, rows_l), at(k, rows_l), zl)
            cross(k)
        yield 2.0
        go_r.wait_recv()
        cross(h, top)
        go_l.wait_recv()
        cross(h, low)
        yield 3.0
        for copy in across:
            copy.wait_recv()
        shared[1] += 1
        if shared[1] == experts:
            place(tgrad_ref, t_all)

    def slot_rows(e):
        hit = ids_ref[...] == e
        chosen = jnp.max(hit.astype(F32), axis=0, keepdims=True)
        weight = jnp.sum(jnp.where(hit, probs_ref[...], 0.0), axis=0, keepdims=True)
        before = lax.broadcasted_iota(jnp.int32, (tok, tok), 0)
        after = lax.broadcasted_iota(jnp.int32, (tok, tok), 1)
        upper = (before <= after).astype(F32).astype(BF)
        count = dot(jnp.broadcast_to(chosen, (16, tok)).astype(BF), upper, NN)[0:1, :]
        place_of = jnp.where(chosen > 0.0, count - 1.0, -1.0).astype(jnp.int32)
        rows = lax.broadcasted_iota(jnp.int32, (slots, tok), 0)
        mine = (jnp.broadcast_to(place_of, (slots, tok)) == rows).astype(F32)
        slot_weight = jnp.sum(mine * weight, axis=1, keepdims=True)
        pick[e] = mine.astype(BF)
        return slot_weight

    part = 512

    def compute():
        weights = []
        for e in range(experts):
            weights.append(slot_rows(e))
            for j in range(0, width, part):
                at = pl.ds(j, part)
                xin[e, :, at] = dot(pick[e], tok_ref[:, at], NN).astype(BF)
                gin[e, :, at] = (dot(pick[e], grad_ref[:, at], NN) * weights[e]).astype(BF)
            clock.busy(3.0)
            yield 0.0
        for e in range(experts):
            while len(from_core[e]) < 10:
                yield 1.0
            yield 2.0
            own_block[e].wait()
            for copy in from_core[e]:
                copy.wait_recv()
            gt[...] = dot(w_all[e, 0], xin[e], NT)
            ut[...] = dot(w_all[e, 1], xin[e], NT)
            clock.busy(1.5)
            yield 0.0
            gate = gt[...]
            sig = 1.0 / (1.0 + jnp.exp(-gate))
            ht[...] = (gate * sig * ut[...]).astype(BF)
            for j in range(0, width, part):
                value = dot(ht[...], w_all[e, 2, :, pl.ds(j, part)], TN) * weights[e]
                for b in range(part // LANE):
                    f = j // LANE + b
                    a0[e, f % NZ, f // NZ] = value[:, b * LANE : (b + 1) * LANE].astype(BF)
            clock.busy(1.5)
            clock.spawn(sum_outputs(e))
            yield 0.0
            back = dot(w_all[e, 2], gin[e], NT)
            gate = gt[...]
            sig = 1.0 / (1.0 + jnp.exp(-gate))
            uat[...] = (back * gate * sig).astype(BF)
            gat[...] = (back * ut[...] * sig * (1.0 + gate * (1.0 - sig))).astype(BF)
            clock.busy(1.5)
            yield 0.0
            for j in range(0, width, part):
                at = pl.ds(j, part)
                value = dot(gat[...], w_all[e, 0, :, at], TN) + dot(uat[...], w_all[e, 1, :, at], TN)
                for b in range(part // LANE):
                    f = j // LANE + b
                    a1[e, f // NZ, f % NZ] = value[:, b * LANE : (b + 1) * LANE].astype(BF)
            clock.busy(1.5)
            clock.spawn(sum_grads(e))
            yield 0.0
            for j in range(0, width, part):
                at = pl.ds(j, part)
                for m, (left, right) in enumerate(((gat, xin), (uat, xin), (ht, gin))):
                    value = dot(left[...], right[e, :, at], NN)
                    for b in range(part // LANE):
                        d = j // LANE + b
                        dw[e, d % 2, d // 4, (d // 2) % 2, m] = value[:, b * LANE : (b + 1) * LANE].astype(BF)
                clock.busy(0.6)
                yield 0.0
            clock.spawn(scatter_grads(e))

    for e in range(experts):
        copy = pltpu.make_async_copy(w_in.at[e], w_block(e, dp), local_sem.at[e])
        copy.start()
        own_block.append(copy)
    clock.spawn(gather_row(0, yh, w_in.at[0]))
    clock.spawn(gather_other(0, 16.0))
    clock.spawn(gather_other(1, 31.0))
    clock.spawn(compute())
    clock.spawn(gather_row(1, yh, w_in.at[1]), 12.0)
    clock.run()
    for copy in sent:
        copy.wait_send()
    assert len(sent) <= NSEM, len(sent)


def body(tokens, expert_ids, route_probs, gate_w, up_w, down_w, out_grad):
    tok, width = tokens.shape
    experts, rows, hid = gate_w.shape
    assert rows == LANE and tok == 512
    slots = tok // 2
    shard = jnp.stack([gate_w.swapaxes(1, 2), up_w.swapaxes(1, 2), down_w], axis=1)
    vmem = pl.BlockSpec(memory_space=pltpu.VMEM)
    two = experts
    scratch = [
        pltpu.VMEM((two, 3, hid, width), BF),
        pltpu.VMEM((two, 2, NX, 2, 3, hid, LANE), BF),
        pltpu.VMEM((two, NX, 2, 3, hid, LANE), BF),
        pltpu.VMEM((two, 2, 2, 3, hid // 2, LANE), BF),
        pltpu.VMEM((two, 2, 2, 3, hid, LANE), BF),
        pltpu.VMEM((two, 3, hid, LANE), BF),
        pltpu.VMEM((two, 3, hid, LANE), BF),
        pltpu.VMEM((two, NZ, 2, slots, LANE), BF),
        pltpu.VMEM((two, 2, NZ, slots, LANE), BF),
        pltpu.VMEM((two, 2, NZ // 2, 2, slots, LANE), BF),
        pltpu.VMEM((two, 2, NZ // 2, slots, LANE), BF),
        pltpu.VMEM((two, slots, LANE), BF),
        pltpu.VMEM((two, slots, LANE), BF),
        pltpu.VMEM((two, NZ, slots, LANE), BF),
        pltpu.VMEM((two, slots, LANE), BF),
        pltpu.VMEM((two, slots, LANE), BF),
        pltpu.VMEM((two, slots, width), BF),
        pltpu.VMEM((two, slots, width), BF),
        pltpu.VMEM((two, slots, tok), BF),
        pltpu.VMEM((two, slots, width), BF),
        pltpu.VMEM((two, slots, width), BF),
        pltpu.VMEM((hid, slots), F32),
        pltpu.VMEM((hid, slots), F32),
        pltpu.VMEM((hid, slots), BF),
        pltpu.VMEM((hid, slots), BF),
        pltpu.VMEM((hid, slots), BF),
        pltpu.SemaphoreType.DMA((NSEM,)),
        pltpu.SemaphoreType.DMA((NSEM,)),
        pltpu.SemaphoreType.DMA((2,)),
    ]
    mixed, token_grad, grads = pl.pallas_call(
        kernel,
        out_shape=(
            jax.ShapeDtypeStruct((tok, width), BF),
            jax.ShapeDtypeStruct((tok, width), BF),
            jax.ShapeDtypeStruct((experts, 3, hid, LANE), BF),
        ),
        in_specs=[vmem] * 5,
        out_specs=(vmem, vmem, vmem),
        scratch_shapes=scratch,
        compiler_params=pltpu.CompilerParams(
            collective_id=0, has_side_effects=True, vmem_limit_bytes=67_043_328
        ),
        name="moe_layer",
    )(shard, tokens, out_grad, expert_ids.T, route_probs.T)
    return (
        mixed,
        token_grad,
        grads[:, 0].swapaxes(1, 2),
        grads[:, 1].swapaxes(1, 2),
        grads[:, 2],
    )


def solution(mesh):
    placed = (
        P("dp", None),
        P("dp", None),
        P("dp", None),
        P(None, "dp", "fsdp"),
        P(None, "dp", "fsdp"),
        P(None, "fsdp", "dp"),
        P("dp", None),
    )
    return jax.shard_map(
        body,
        mesh=mesh,
        in_specs=placed,
        out_specs=(
            P("dp", None),
            P("dp", None),
            P(None, "dp", "fsdp"),
            P(None, "dp", "fsdp"),
            P(None, "fsdp", "dp"),
        ),
        check_vma=False,
    )
```
